32 devices in a mesh: groups: 2 (over y), ctx: 4 (over z), head: 2 (over x), rep: 2 (over core).
Axes of the slice: x: 2, y: 2, z: 4, core: 2. Of those that a mesh axis runs over, the one named last changes fastest.
Arguments:
- queries: bfloat16 [12288, 1536], P(('groups', 'ctx', 'rep'), 'head'), parts along dimension 0, may hold values from -5 to 5
- keys_in: bfloat16 [12288, 1536], P(('groups', 'ctx', 'rep'), 'head'), parts along dimension 0, may hold values from -12 to 12
- values: bfloat16 [12288, 1536], P(('groups', 'ctx', 'rep'), 'head'), parts along dimension 0, may hold values from -6 to 6
- grad_out: bfloat16 [12288, 1536], P(('groups', 'ctx', 'rep'), 'head'), parts along dimension 0, may hold values from -6 to 6
- clip_ids: int32 [16], P('groups'), parts along dimension 0, may hold values from 0 to 2, as said below
Outputs:
- grad_query: bfloat16 [12288, 1536], P(('groups', 'ctx', 'rep'), 'head'), parts along dimension 0
- grad_key: bfloat16 [12288, 1536], P(('groups', 'ctx', 'rep'), 'head'), parts along dimension 0
- grad_value: bfloat16 [12288, 1536], P(('groups', 'ctx', 'rep'), 'head'), parts along dimension 0
The draws below stay inside these ranges and needn't reach their ends.
There are 2 independent parts, one for each index of `groups`. The reference program is written for one: setup_inputs(seed, part) draws one part's arguments, and reference() takes and returns one part's arrays. A program takes and returns all parts, laid end to end along the dimension named above; each array names one. Nothing has to cross between parts.
Inputs may be any that keep to these rules, and one draw needn't show every extreme that they name: clip_ids of the first tile row is 0, and each next tile row's id equals the previous one or exceeds it by one; a clip is the run of tile rows with one id; the last tile row's id is 2.
All inputs are finite; a program needn't handle non-finite values.
Results may differ from the reference program's by a relative error of at most 0.013.
Values may be sent and summed in bfloat16 or wider, within the bound.
A program may use at most 64 MiB of HBM per device.

```python
import math
import jax
import jax.numpy as jnp
from jax import lax

HEADS = 12
HEAD_DIM = 128
WIDTH = 1536
ROW_TOK = 768
ROWS = 8
TOKENS = 6144


def shared_pair(key):
    base_key = jax.random.fold_in(key, 11)
    first_key = jax.random.fold_in(base_key, 0)
    second_key = jax.random.fold_in(base_key, 1)
    third_key = jax.random.fold_in(base_key, 2)
    fifth_key = jax.random.fold_in(base_key, 4)
    sixth_key = jax.random.fold_in(base_key, 5)
    seventh_key = jax.random.fold_in(base_key, 6)
    shape = (TOKENS, WIDTH)
    query_vals = jnp.clip(jax.random.normal(first_key, shape, jnp.float32), -4.0, 4.0)
    key_vals = jnp.clip(jax.random.normal(second_key, shape, jnp.float32), -4.0, 4.0)
    row_scales = jnp.exp(jax.random.uniform(third_key, (TOKENS, 1), jnp.float32, math.log(0.5), math.log(1.5)))
    key_vals = key_vals * row_scales
    positions = jnp.arange(TOKENS)
    offset = jax.random.randint(fifth_key, (), 0, 53)
    paired = ((positions + offset) % 53 == 0) & (positions % ROW_TOK < ROW_TOK - 1)
    pattern = jnp.where(jax.random.normal(sixth_key, shape, jnp.float32) > 0.0, 1.0, -1.0)
    rough = jax.random.uniform(seventh_key, shape, jnp.float32, 0.7, 1.3)
    query_vals = jnp.where(paired[:, None], 2.5 * pattern, query_vals)
    partner = jnp.roll(paired, 1)
    key_vals = jnp.where(partner[:, None], 0.6 * jnp.roll(pattern, 1, axis=0) * rough, key_vals)
    return (query_vals, key_vals)


def draw_queries(key, part):
    return shared_pair(key)[0].astype(jnp.bfloat16)


def draw_keys_in(key, part):
    return shared_pair(key)[1].astype(jnp.bfloat16)


def draw_clip_ids(key, part):
    order = jax.random.permutation(jax.random.fold_in(key, 5), ROWS - 1).astype(jnp.int32) + 1
    picked = order[:2]
    fresh = jnp.zeros((ROWS,), jnp.int32).at[picked].set(1)
    return jnp.cumsum(fresh).astype(jnp.int32)


def level_of(rng, shape, cuts, least, top_value):
    level, own = 1.0, jax.random.fold_in(rng, 6)
    for position, shards_of in cuts:
        heights = jnp.exp(jax.random.uniform(jax.random.fold_in(own, position), (shards_of,), jnp.float32, least / len(cuts), top_value / len(cuts)))
        level = level * jnp.repeat(heights, shape[position] // shards_of).reshape([-1 if axis == position else 1 for axis in range(len(shape))])
    return level


def normal_values(own_key, shape, scale, limit, cuts=(), kind=jnp.bfloat16):
    drawn = jax.random.normal(own_key, shape, jnp.float32) * scale
    if len(cuts) > 0:
        drawn = level_of(own_key, shape, cuts, -0.22, 0.18) * drawn
    return jnp.clip(drawn, min=-limit, max=limit).astype(kind)


def setup_inputs(seed: int = 0, part: int = 0) -> dict:
    key_list = jax.random.split(jax.random.key(seed), 6)
    own_keys = jax.random.split(jax.random.fold_in(key_list[5], part), 6)
    return {
        "queries": draw_queries(jax.random.fold_in(jax.random.fold_in(key_list[5], part), 71), part),
        "keys_in": draw_keys_in(jax.random.fold_in(jax.random.fold_in(key_list[5], part), 71), part),
        "values": normal_values(own_keys[2], (TOKENS, WIDTH), 1.0, 6.0, ((0, 8), (1, 2))),
        "grad_out": normal_values(own_keys[3], (TOKENS, WIDTH), 1.0, 6.0, ((0, 8), (1, 2))),
        "clip_ids": draw_clip_ids(jax.random.fold_in(jax.random.fold_in(key_list[5], part), 71), part),
    }


def reference(queries, keys_in, values, grad_out, clip_ids):
    row_count = clip_ids.shape[0]
    row_tok = queries.shape[0] // row_count
    feature_width = queries.shape[1]
    softmax_scale = HEAD_DIM ** -0.5

    def by_rows(array):
        return array.reshape(row_count, row_tok, HEADS, HEAD_DIM)

    query_rows = by_rows(queries)
    grad_rows = by_rows(grad_out)
    zero_row = jnp.zeros((1, row_tok, HEADS, HEAD_DIM), jnp.bfloat16)
    key_padded = jnp.concatenate([zero_row, by_rows(keys_in), zero_row], axis=0)
    value_padded = jnp.concatenate([zero_row, by_rows(values), zero_row], axis=0)
    sentinel = jnp.full((1,), -1, jnp.int32)
    clip_padded = jnp.concatenate([sentinel, clip_ids.astype(jnp.int32), sentinel], axis=0)

    def one_row(row_index):
        query_now = query_rows[row_index].astype(jnp.float32)
        grad_now = grad_rows[row_index].astype(jnp.float32)
        key_window = lax.dynamic_slice_in_dim(key_padded, row_index, 3, 0)
        value_window = lax.dynamic_slice_in_dim(value_padded, row_index, 3, 0)
        clip_window = lax.dynamic_slice_in_dim(clip_padded, row_index, 3, 0)
        own_clip = clip_ids[row_index]
        key_mask = jnp.repeat(clip_window == own_clip, row_tok)
        key_flat = key_window.reshape(3 * row_tok, HEADS, HEAD_DIM).astype(jnp.float32)
        value_flat = value_window.reshape(3 * row_tok, HEADS, HEAD_DIM).astype(jnp.float32)
        scores = jnp.einsum("qhd,khd->hqk", query_now, key_flat) * softmax_scale
        scores = jnp.where(key_mask[None, None, :], scores, -jnp.inf)
        row_max = jnp.max(scores, axis=2, keepdims=True)
        log_total = row_max + jnp.log(jnp.sum(jnp.exp(scores - row_max), axis=2, keepdims=True))
        probs = jnp.exp(scores - log_total)
        probs_low = probs.astype(jnp.bfloat16)
        dprob = jnp.einsum("qhd,khd->hqk", grad_now, value_flat)
        row_delta = jnp.sum(probs * dprob, axis=2, keepdims=True)
        dscores = (probs * (dprob - row_delta)).astype(jnp.bfloat16)
        dscores_wide = dscores.astype(jnp.float32)
        grad_q = jnp.einsum("hqk,khd->qhd", dscores_wide, key_flat) * softmax_scale
        key_terms = jnp.einsum("hqk,qhd->khd", dscores_wide, query_now) * softmax_scale
        value_terms = jnp.einsum("hqk,qhd->khd", probs_low.astype(jnp.float32), grad_now)
        return (grad_q.astype(jnp.bfloat16).reshape(row_tok, feature_width),
                key_terms.astype(jnp.bfloat16).reshape(3, row_tok, feature_width),
                value_terms.astype(jnp.bfloat16).reshape(3, row_tok, feature_width))

    grad_q_rows, key_terms, value_terms = lax.map(one_row, jnp.arange(row_count, dtype=jnp.int32))

    def combine(block_terms):
        block_terms = block_terms.astype(jnp.float32)
        empty_row = jnp.zeros((1, row_tok, feature_width), jnp.float32)
        from_upper = jnp.concatenate([block_terms[1:, 0], empty_row], axis=0)
        from_lower = jnp.concatenate([empty_row, block_terms[:-1, 2]], axis=0)
        summed = block_terms[:, 1] + from_upper + from_lower
        return summed.astype(jnp.bfloat16).reshape(row_count * row_tok, feature_width)

    grad_query = grad_q_rows.reshape(row_count * row_tok, feature_width)
    return (grad_query, combine(key_terms), combine(value_terms))
```

```python
import functools
import math

import jax
import jax.numpy as jnp
from jax import lax
from jax.experimental import pallas as pl
from jax.experimental.pallas import tpu as pltpu
from jax.sharding import PartitionSpec as P

HEAD_DIM = 128
QUERY_TILE = 256
SCALE = HEAD_DIM ** -0.5
SCALE_LOG2 = SCALE * math.log2(math.e)
MESH = pl.DeviceIdType.MESH


def nt_product(left, right):
    return lax.dot_general(
        left, right, (((1,), (1,)), ((), ())), preferred_element_type=jnp.float32
    )


def tn_product(left, right):
    return lax.dot_general(
        left, right, (((0,), (0,)), ((), ())), preferred_element_type=jnp.float32
    )


def nn_product(left, right):
    return jnp.dot(left, right, preferred_element_type=jnp.float32)


def attention_kernel(
    bias_ref, q_hbm, k_hbm, v_hbm, g_hbm, dq_hbm, dk_hbm, dv_hbm,
    q_all, g_all, k_all, v_all, sent, got, own, dq_all, acc,
    load_sem, kv_send, kv_recv, term_send, term_recv, out_sem,
):
    row_tok, width = q_all.shape
    heads = width // HEAD_DIM
    reps = lax.axis_size("rep")
    count = lax.axis_size("ctx") * reps
    position = lax.axis_index("ctx") * reps + lax.axis_index("rep")
    has_low, has_high = position > 0, position < count - 1

    def device(index):
        return {"ctx": index // reps, "rep": lax.rem(index, reps)}

    high = device(jnp.minimum(position + 1, count - 1))
    low = device(jnp.maximum(position - 1, 0))
    targets = (high, low)
    sends = (has_high, has_low)
    receives = (has_low, has_high)

    def strip(head):
        return pl.ds(pl.multiple_of(head * HEAD_DIM, HEAD_DIM), HEAD_DIM)

    def kv_copies(head, way):
        columns = strip(head)
        return [
            pltpu.make_async_remote_copy(
                src_ref=source.at[:, columns],
                dst_ref=target.at[2 * way, :, columns],
                send_sem=kv_send.at[way, head, which],
                recv_sem=kv_recv.at[way, head, which],
                device_id=targets[way],
                device_id_type=MESH,
            )
            for which, (source, target) in enumerate(((k_hbm, k_all), (v_hbm, v_all)))
        ]

    def term_copy(head, way):
        columns = strip(head)
        return pltpu.make_async_remote_copy(
            src_ref=sent.at[way, :, :, columns],
            dst_ref=got.at[way, :, :, columns],
            send_sem=term_send.at[way, head],
            recv_sem=term_recv.at[way, head],
            device_id=targets[way],
            device_id_type=MESH,
        )

    def out_copy(head, which):
        columns = strip(head)
        source = (dq_all, own.at[0], own.at[1])[which]
        target = (dq_hbm, dk_hbm, dv_hbm)[which]
        return pltpu.make_async_copy(
            source.at[:, columns], target.at[:, columns], out_sem.at[which, head]
        )

    def send_kv(head):
        for way in range(2):
            @pl.when(sends[way])
            def _():
                for copy in kv_copies(head, way):
                    copy.start()

    loads = [
        pltpu.make_async_copy(source, target, load_sem.at[index])
        for index, (source, target) in enumerate(
            ((q_hbm, q_all), (k_hbm, k_all.at[1]), (v_hbm, v_all.at[1]), (g_hbm, g_all))
        )
    ]
    barrier = pltpu.get_barrier_semaphore()
    for way in range(2):
        @pl.when(sends[way])
        def _():
            pl.semaphore_signal(barrier, inc=1, device_id=targets[way], device_id_type=MESH)
    for load in loads:
        load.start()
    pl.semaphore_wait(barrier, has_low.astype(jnp.int32) + has_high.astype(jnp.int32))
    for head in range(min(2, heads)):
        send_kv(head)
    for way in range(2):
        @pl.when(jnp.logical_not(receives[way]))
        def _():
            k_all[2 * way] = jnp.zeros((row_tok, width), jnp.bfloat16)
            v_all[2 * way] = jnp.zeros((row_tok, width), jnp.bfloat16)
            got[way] = jnp.zeros((2, row_tok, width), jnp.bfloat16)
    for load in loads:
        load.wait()

    biases = (bias_ref[0], bias_ref[1], bias_ref[2])

    def combine(head):
        columns = strip(head)
        for way in range(2):
            @pl.when(receives[way])
            def _():
                term_copy(head, way).wait_recv()
        for which in range(2):
            total = own[which, :, columns].astype(jnp.float32)
            for way in range(2):
                total = total + got[way, which, :, columns].astype(jnp.float32)
            own[which, :, columns] = total.astype(jnp.bfloat16)
            out_copy(head, 1 + which).start()

    def one_head(head, carry):
        columns = strip(head)
        for way in range(2):
            @pl.when(receives[way])
            def _():
                for copy in kv_copies(head, way):
                    copy.wait_recv()

        @pl.when(head + 2 < heads)
        def _():
            send_kv(head + 2)

        acc[...] = jnp.zeros_like(acc)

        def one_tile(tile, inner):
            rows = pl.ds(pl.multiple_of(tile * QUERY_TILE, QUERY_TILE), QUERY_TILE)
            q_tile = q_all[rows, columns]
            g_tile = g_all[rows, columns]
            scores = [nt_product(k_all[b, :, columns], q_tile) for b in range(3)]
            tops = [
                jnp.max(scores[b], axis=0, keepdims=True) + biases[b] for b in range(3)
            ]
            top = jnp.maximum(jnp.maximum(tops[0], tops[1]), tops[2])
            weights = [
                jnp.exp2(scores[b] * SCALE_LOG2 - (top - biases[b]) * SCALE_LOG2)
                for b in range(3)
            ]
            total = sum(jnp.sum(w, axis=0, keepdims=True) for w in weights)
            inverse = 1.0 / total
            dprobs = [nt_product(v_all[b, :, columns], g_tile) for b in range(3)]
            delta = inverse * sum(
                jnp.sum(w * d, axis=0, keepdims=True) for w, d in zip(weights, dprobs)
            )
            dq_tile = jnp.zeros((QUERY_TILE, HEAD_DIM), jnp.float32)
            for b in range(3):
                keys = pl.ds(b * row_tok, row_tok)
                probs = weights[b] * inverse
                dscores = (probs * (dprobs[b] - delta)).astype(jnp.bfloat16)
                acc[1, keys, :] += nn_product(probs.astype(jnp.bfloat16), g_tile)
                acc[0, keys, :] += nn_product(dscores, q_tile)
                dq_tile = dq_tile + tn_product(dscores, k_all[b, :, columns])
            dq_all[rows, columns] = (dq_tile * SCALE).astype(jnp.bfloat16)
            return inner

        lax.fori_loop(0, row_tok // QUERY_TILE, one_tile, 0)
        for which in range(2):
            factor = (SCALE, 1.0)[which]
            for b in range(3):
                block = acc[which, b * row_tok : (b + 1) * row_tok, :] * factor
                block = block.astype(jnp.bfloat16)
                if b == 1:
                    own[which, :, columns] = block
                else:
                    sent[1 - b // 2, which, :, columns] = block
        for way in range(2):
            @pl.when(sends[way])
            def _():
                term_copy(head, way).start()
        out_copy(head, 0).start()

        @pl.when(head >= 2)
        def _():
            combine(head - 2)

        return carry

    lax.fori_loop(0, heads, one_head, 0)
    for head in range(max(heads - 2, 0), heads):
        combine(head)

    def finish(head, carry):
        for way in range(2):
            @pl.when(sends[way])
            def _():
                for copy in kv_copies(head, way):
                    copy.wait_send()
                term_copy(head, way).wait_send()
        for which in range(3):
            out_copy(head, which).wait()
        return carry

    lax.fori_loop(0, heads, finish, 0)


def per_device(queries, keys_in, values, grad_out, clip_ids):
    row_tok, width = queries.shape
    heads = width // HEAD_DIM
    position = lax.axis_index(("ctx", "rep"))
    row_count = lax.axis_size(("ctx", "rep"))
    around = position + jnp.arange(-1, 2, dtype=jnp.int32)
    inside = (around >= 0) & (around < row_count)
    clips = clip_ids[jnp.clip(around, 0, row_count - 1)]
    bias = jnp.where(inside & (clips == clips[1]), 0.0, -jnp.inf).astype(jnp.float32)
    shape = jax.ShapeDtypeStruct((row_tok, width), jnp.bfloat16)
    anywhere = pl.BlockSpec(memory_space=pl.ANY)
    low = jnp.bfloat16
    return pl.pallas_call(
        attention_kernel,
        out_shape=(shape, shape, shape),
        in_specs=[pl.BlockSpec(memory_space=pltpu.SMEM)] + [anywhere] * 4,
        out_specs=(anywhere, anywhere, anywhere),
        scratch_shapes=[
            pltpu.VMEM((row_tok, width), low),
            pltpu.VMEM((row_tok, width), low),
            pltpu.VMEM((3, row_tok, width), low),
            pltpu.VMEM((3, row_tok, width), low),
            pltpu.VMEM((2, 2, row_tok, width), low),
            pltpu.VMEM((2, 2, row_tok, width), low),
            pltpu.VMEM((2, row_tok, width), low),
            pltpu.VMEM((row_tok, width), low),
            pltpu.VMEM((2, 3 * row_tok, HEAD_DIM), jnp.float32),
            pltpu.SemaphoreType.DMA((4,)),
            pltpu.SemaphoreType.DMA((2, heads, 2)),
            pltpu.SemaphoreType.DMA((2, heads, 2)),
            pltpu.SemaphoreType.DMA((2, heads)),
            pltpu.SemaphoreType.DMA((2, heads)),
            pltpu.SemaphoreType.DMA((3, heads)),
        ],
        compiler_params=pltpu.CompilerParams(
            collective_id=0, has_side_effects=True, vmem_limit_bytes=58 * 1024 * 1024
        ),
    )(bias, queries, keys_in, values, grad_out)


def solution(mesh):
    tokens = P(("groups", "ctx", "rep"), "head")
    return jax.shard_map(
        per_device,
        mesh=mesh,
        in_specs=(tokens, tokens, tokens, tokens, P("groups")),
        out_specs=(tokens, tokens, tokens),
        check_vma=False,
    )
```

```python
import functools
import math

import jax
import jax.numpy as jnp
from jax import lax
from jax.experimental import pallas as pl
from jax.experimental.pallas import tpu as pltpu
from jax.sharding import PartitionSpec as P

HEAD_DIM = 128
KEY_CHUNK = 32
LANES = 8
SCALE = HEAD_DIM ** -0.5
SCALE_LOG2 = SCALE * math.log2(math.e)
MESH = pl.DeviceIdType.MESH


def nt_product(left, right):
    return lax.dot_general(
        left, right, (((1,), (1,)), ((), ())), preferred_element_type=jnp.float32
    )


def tn_product(left, right):
    return lax.dot_general(
        left, right, (((0,), (0,)), ((), ())), preferred_element_type=jnp.float32
    )


def nn_product(left, right):
    return jnp.dot(left, right, preferred_element_type=jnp.float32)


def attention_kernel(
    clip_ref, q_hbm, k_hbm, v_hbm, g_hbm, dq_hbm, dk_hbm, dv_hbm,
    q_all, g_all, k_all, v_all, sent, got, own, dq_all,
    weights, dprobs, probs_low, dscores,
    load_sem, kv_send, kv_recv, term_send, term_recv, out_sem,
):
    row_tok, width = q_all.shape
    heads = width // HEAD_DIM
    reps = lax.axis_size("rep")
    count = lax.axis_size("ctx") * reps
    position = lax.axis_index("ctx") * reps + lax.axis_index("rep")
    has_low, has_high = position > 0, position < count - 1

    def device(index):
        return {"ctx": index // reps, "rep": lax.rem(index, reps)}

    high = device(jnp.minimum(position + 1, count - 1))
    low = device(jnp.maximum(position - 1, 0))
    targets = (high, low)
    sends = (has_high, has_low)
    receives = (has_low, has_high)

    def strip(head):
        return pl.ds(pl.multiple_of(head * HEAD_DIM, HEAD_DIM), HEAD_DIM)

    def kv_copies(head, way):
        columns = strip(head)
        return [
            pltpu.make_async_remote_copy(
                src_ref=source.at[:, columns],
                dst_ref=target.at[2 * way, :, columns],
                send_sem=kv_send.at[way, head, which],
                recv_sem=kv_recv.at[way, head, which],
                device_id=targets[way],
                device_id_type=MESH,
            )
            for which, (source, target) in enumerate(((k_hbm, k_all), (v_hbm, v_all)))
        ]

    def term_copy(head, way):
        columns = strip(head)
        return pltpu.make_async_remote_copy(
            src_ref=sent.at[way, :, :, columns],
            dst_ref=got.at[way, :, :, columns],
            send_sem=term_send.at[way, head],
            recv_sem=term_recv.at[way, head],
            device_id=targets[way],
            device_id_type=MESH,
        )

    def out_copy(head, which):
        columns = strip(head)
        source = (dq_all, own.at[0], own.at[1])[which]
        target = (dq_hbm, dk_hbm, dv_hbm)[which]
        return pltpu.make_async_copy(
            source.at[:, columns], target.at[:, columns], out_sem.at[which, head]
        )

    def send_kv(head):
        for way in range(2):
            @pl.when(sends[way])
            def _():
                for copy in kv_copies(head, way):
                    copy.start()

    loads = [
        pltpu.make_async_copy(source, target, load_sem.at[index])
        for index, (source, target) in enumerate(
            ((q_hbm, q_all), (k_hbm, k_all.at[1]), (v_hbm, v_all.at[1]), (g_hbm, g_all))
        )
    ]
    barrier = pltpu.get_barrier_semaphore()
    for way in range(2):
        @pl.when(sends[way])
        def _():
            pl.semaphore_signal(barrier, inc=1, device_id=targets[way], device_id_type=MESH)
    for load in loads:
        load.start()
    pl.semaphore_wait(barrier, has_low.astype(jnp.int32) + has_high.astype(jnp.int32))
    for head in range(min(2, heads)):
        send_kv(head)
    for way in range(2):
        @pl.when(jnp.logical_not(receives[way]))
        def _():
            k_all[2 * way] = jnp.zeros((row_tok, width), jnp.bfloat16)
            v_all[2 * way] = jnp.zeros((row_tok, width), jnp.bfloat16)
            got[way] = jnp.zeros((2, row_tok, width), jnp.bfloat16)
    for load in loads:
        load.wait()

    own_clip = clip_ref[position]
    low_clip = clip_ref[jnp.maximum(position - 1, 0)]
    high_clip = clip_ref[jnp.minimum(position + 1, count - 1)]
    biases = (
        jnp.where(has_low & (low_clip == own_clip), 0.0, -jnp.inf),
        0.0,
        jnp.where(has_high & (high_clip == own_clip), 0.0, -jnp.inf),
    )

    def combine(head):
        columns = strip(head)
        for way in range(2):
            @pl.when(receives[way])
            def _():
                term_copy(head, way).wait_recv()
        for which in range(2):
            total = own[which, :, columns].astype(jnp.float32)
            for way in range(2):
                total = total + got[way, which, :, columns].astype(jnp.float32)
            own[which, :, columns] = total.astype(jnp.bfloat16)
            out_copy(head, 1 + which).start()

    def one_head(head, carry):
        columns = strip(head)
        for way in range(2):
            @pl.when(receives[way])
            def _():
                for copy in kv_copies(head, way):
                    copy.wait_recv()

        @pl.when(head + 2 < heads)
        def _():
            send_kv(head + 2)

        q_head, g_head = q_all[:, columns], g_all[:, columns]
        chunks = [pl.ds(start, KEY_CHUNK) for start in range(0, row_tok, KEY_CHUNK)]

        def folded(value, op):
            return op(value.reshape(KEY_CHUNK // LANES, LANES, row_tok), axis=0)

        top = None
        for b in range(3):
            weights[b] = nt_product(k_all[b, :, columns], q_head)
            block_top = None
            for chunk in chunks:
                part = folded(weights[b, chunk, :], jnp.max)
                block_top = part if block_top is None else jnp.maximum(block_top, part)
            block_top = jnp.max(block_top, axis=0, keepdims=True) + biases[b]
            top = block_top if top is None else jnp.maximum(top, block_top)
        total = jnp.zeros((LANES, row_tok), jnp.float32)
        delta = jnp.zeros((LANES, row_tok), jnp.float32)
        for b in range(3):
            dprobs[b] = nt_product(v_all[b, :, columns], g_head)
            shift = (top - biases[b]) * SCALE_LOG2
            for chunk in chunks:
                weight = jnp.exp2(weights[b, chunk, :] * SCALE_LOG2 - shift)
                weights[b, chunk, :] = weight
                total = total + folded(weight, jnp.sum)
                delta = delta + folded(weight * dprobs[b, chunk, :], jnp.sum)
        inverse = 1.0 / jnp.sum(total, axis=0, keepdims=True)
        delta = inverse * jnp.sum(delta, axis=0, keepdims=True)
        dq_head = None
        for b in (0, 2, 1):
            for chunk in chunks:
                probs = weights[b, chunk, :] * inverse
                probs_low[b, chunk, :] = probs.astype(jnp.bfloat16)
                dscores[b, chunk, :] = (probs * (dprobs[b, chunk, :] - delta)).astype(
                    jnp.bfloat16
                )
            value_term = nn_product(probs_low[b], g_head).astype(jnp.bfloat16)
            key_term = (nn_product(dscores[b], q_head) * SCALE).astype(jnp.bfloat16)
            part = tn_product(dscores[b], k_all[b, :, columns])
            dq_head = part if dq_head is None else dq_head + part
            if b == 1:
                own[0, :, columns] = key_term
                own[1, :, columns] = value_term
            else:
                sent[1 - b // 2, 0, :, columns] = key_term
                sent[1 - b // 2, 1, :, columns] = value_term
        dq_all[:, columns] = (dq_head * SCALE).astype(jnp.bfloat16)
        for way in range(2):
            @pl.when(sends[way])
            def _():
                term_copy(head, way).start()
        out_copy(head, 0).start()

        @pl.when(head >= 2)
        def _():
            combine(head - 2)

        return carry

    lax.fori_loop(0, heads, one_head, 0)
    for head in range(max(heads - 2, 0), heads):
        combine(head)

    def finish(head, carry):
        for way in range(2):
            @pl.when(sends[way])
            def _():
                for copy in kv_copies(head, way):
                    copy.wait_send()
                term_copy(head, way).wait_send()
        for which in range(3):
            out_copy(head, which).wait()
        return carry

    lax.fori_loop(0, heads, finish, 0)


def per_device(queries, keys_in, values, grad_out, clip_ids):
    row_tok, width = queries.shape
    heads = width // HEAD_DIM
    shape = jax.ShapeDtypeStruct((row_tok, width), jnp.bfloat16)
    anywhere = pl.BlockSpec(memory_space=pl.ANY)
    low = jnp.bfloat16
    return pl.pallas_call(
        attention_kernel,
        out_shape=(shape, shape, shape),
        in_specs=[pl.BlockSpec(memory_space=pltpu.SMEM)] + [anywhere] * 4,
        out_specs=(anywhere, anywhere, anywhere),
        scratch_shapes=[
            pltpu.VMEM((row_tok, width), low),
            pltpu.VMEM((row_tok, width), low),
            pltpu.VMEM((3, row_tok, width), low),
            pltpu.VMEM((3, row_tok, width), low),
            pltpu.VMEM((2, 2, row_tok, width), low),
            pltpu.VMEM((2, 2, row_tok, width), low),
            pltpu.VMEM((2, row_tok, width), low),
            pltpu.VMEM((row_tok, width), low),
            pltpu.VMEM((3, row_tok, row_tok), jnp.float32),
            pltpu.VMEM((3, row_tok, row_tok), jnp.float32),
            pltpu.VMEM((3, row_tok, row_tok), low),
            pltpu.VMEM((3, row_tok, row_tok), low),
            pltpu.SemaphoreType.DMA((4,)),
            pltpu.SemaphoreType.DMA((2, heads, 2)),
            pltpu.SemaphoreType.DMA((2, heads, 2)),
            pltpu.SemaphoreType.DMA((2, heads)),
            pltpu.SemaphoreType.DMA((2, heads)),
            pltpu.SemaphoreType.DMA((3, heads)),
        ],
        compiler_params=pltpu.CompilerParams(
            collective_id=0, has_side_effects=True, vmem_limit_bytes=58 * 1024 * 1024
        ),
    )(clip_ids, queries, keys_in, values, grad_out)


def solution(mesh):
    tokens = P(("groups", "ctx", "rep"), "head")
    return jax.shard_map(
        per_device,
        mesh=mesh,
        in_specs=(tokens, tokens, tokens, tokens, P("groups")),
        out_specs=(tokens, tokens, tokens),
        check_vma=False,
    )
```

```python
import functools
import math

import jax
import jax.numpy as jnp
from jax import lax
from jax.experimental import pallas as pl
from jax.experimental.pallas import tpu as pltpu
from jax.sharding import PartitionSpec as P

HEAD_DIM = 128
KEY_CHUNK = 32
LANES = 8
SCALE = HEAD_DIM ** -0.5
SCALE_LOG2 = SCALE * math.log2(math.e)
MESH = pl.DeviceIdType.MESH


def nt_product(left, right):
    return lax.dot_general(
        left, right, (((1,), (1,)), ((), ())), preferred_element_type=jnp.float32
    )


def tn_product(left, right):
    return lax.dot_general(
        left, right, (((0,), (0,)), ((), ())), preferred_element_type=jnp.float32
    )


def nn_product(left, right):
    return jnp.dot(left, right, preferred_element_type=jnp.float32)


def attention_kernel(
    clip_ref, q_hbm, k_hbm, v_hbm, g_hbm, dq_hbm, dk_hbm, dv_hbm,
    q_all, g_all, k_all, v_all, sent, got, own, dq_all,
    weights, dprobs, probs_low, dscores,
    load_sem, kv_send, kv_recv, term_send, term_recv, out_sem,
):
    heads, row_tok, _ = q_all.shape
    reps = lax.axis_size("rep")
    count = lax.axis_size("ctx") * reps
    position = lax.axis_index("ctx") * reps + lax.axis_index("rep")
    has_low, has_high = position > 0, position < count - 1

    def device(index):
        return {"ctx": index // reps, "rep": lax.rem(index, reps)}

    high = device(jnp.minimum(position + 1, count - 1))
    low = device(jnp.maximum(position - 1, 0))
    targets = (high, low)
    sends = (has_high, has_low)
    receives = (has_low, has_high)

    def strip(head):
        return pl.ds(pl.multiple_of(head * HEAD_DIM, HEAD_DIM), HEAD_DIM)

    def kv_copies(head, way):
        return [
            pltpu.make_async_remote_copy(
                src_ref=target.at[1, head],
                dst_ref=target.at[2 * way, head],
                send_sem=kv_send.at[way, head, which],
                recv_sem=kv_recv.at[way, head, which],
                device_id=targets[way],
                device_id_type=MESH,
            )
            for which, target in enumerate((k_all, v_all))
        ]

    def term_copy(head, way):
        return pltpu.make_async_remote_copy(
            src_ref=sent.at[way, head],
            dst_ref=got.at[way, head],
            send_sem=term_send.at[way, head],
            recv_sem=term_recv.at[way, head],
            device_id=targets[way],
            device_id_type=MESH,
        )

    def out_copy(head, which):
        columns = strip(head)
        source = (dq_all.at[head], own.at[0, head], own.at[1, head])[which]
        target = (dq_hbm, dk_hbm, dv_hbm)[which]
        return pltpu.make_async_copy(
            source, target.at[:, columns], out_sem.at[which, head]
        )

    def send_kv(head):
        for way in range(2):
            @pl.when(sends[way])
            def _():
                for copy in kv_copies(head, way):
                    copy.start()

    def loads(head):
        columns = strip(head)
        return [
            pltpu.make_async_copy(source.at[:, columns], target, load_sem.at[index, head])
            for index, (source, target) in enumerate(
                (
                    (k_hbm, k_all.at[1, head]),
                    (v_hbm, v_all.at[1, head]),
                    (q_hbm, q_all.at[head]),
                    (g_hbm, g_all.at[head]),
                )
            )
        ]

    barrier = pltpu.get_barrier_semaphore()
    for way in range(2):
        @pl.when(sends[way])
        def _():
            pl.semaphore_signal(barrier, inc=1, device_id=targets[way], device_id_type=MESH)
    for head in range(heads):
        for load in loads(head):
            load.start()
    pl.semaphore_wait(barrier, has_low.astype(jnp.int32) + has_high.astype(jnp.int32))
    for head in range(heads):
        for load in loads(head)[:2]:
            load.wait()
        if head < 2:
            send_kv(head)
    for way in range(2):
        @pl.when(jnp.logical_not(receives[way]))
        def _():
            k_all[2 * way] = jnp.zeros((heads, row_tok, HEAD_DIM), jnp.bfloat16)
            v_all[2 * way] = jnp.zeros((heads, row_tok, HEAD_DIM), jnp.bfloat16)
            got[way] = jnp.zeros((heads, 2, row_tok, HEAD_DIM), jnp.bfloat16)
    for head in range(heads):
        for load in loads(head)[2:]:
            load.wait()

    own_clip = clip_ref[position]
    low_clip = clip_ref[jnp.maximum(position - 1, 0)]
    high_clip = clip_ref[jnp.minimum(position + 1, count - 1)]
    biases = (
        jnp.where(has_low & (low_clip == own_clip), 0.0, -jnp.inf),
        0.0,
        jnp.where(has_high & (high_clip == own_clip), 0.0, -jnp.inf),
    )

    def combine(head):
        for way in range(2):
            @pl.when(receives[way])
            def _():
                term_copy(head, way).wait_recv()
        for which in range(2):
            total = own[which, head].astype(jnp.float32)
            for way in range(2):
                total = total + got[way, head, which].astype(jnp.float32)
            own[which, head] = total.astype(jnp.bfloat16)
            out_copy(head, 1 + which).start()

    def one_head(head, carry):
        for way in range(2):
            @pl.when(receives[way])
            def _():
                for copy in kv_copies(head, way):
                    copy.wait_recv()

        @pl.when(head + 2 < heads)
        def _():
            send_kv(head + 2)

        q_head, g_head = q_all[head], g_all[head]
        chunks = [pl.ds(start, KEY_CHUNK) for start in range(0, row_tok, KEY_CHUNK)]

        def folded(value, op):
            return op(value.reshape(KEY_CHUNK // LANES, LANES, row_tok), axis=0)

        top = None
        for b in range(3):
            weights[b] = nt_product(k_all[b, head], q_head)
            block_top = None
            for chunk in chunks:
                part = folded(weights[b, chunk, :], jnp.max)
                block_top = part if block_top is None else jnp.maximum(block_top, part)
            block_top = jnp.max(block_top, axis=0, keepdims=True) + biases[b]
            top = block_top if top is None else jnp.maximum(top, block_top)
        total = jnp.zeros((LANES, row_tok), jnp.float32)
        delta = jnp.zeros((LANES, row_tok), jnp.float32)
        for b in range(3):
            dprobs[b] = nt_product(v_all[b, head], g_head)
            shift = (top - biases[b]) * SCALE_LOG2
            for chunk in chunks:
                weight = jnp.exp2(weights[b, chunk, :] * SCALE_LOG2 - shift)
                weights[b, chunk, :] = weight
                total = total + folded(weight, jnp.sum)
                delta = delta + folded(weight * dprobs[b, chunk, :], jnp.sum)
        inverse = 1.0 / jnp.sum(total, axis=0, keepdims=True)
        delta = inverse * jnp.sum(delta, axis=0, keepdims=True)
        dq_head = None
        for b in (0, 2, 1):
            for chunk in chunks:
                probs = weights[b, chunk, :] * inverse
                probs_low[b, chunk, :] = probs.astype(jnp.bfloat16)
                dscores[b, chunk, :] = (probs * (dprobs[b, chunk, :] - delta)).astype(
                    jnp.bfloat16
                )
            value_term = nn_product(probs_low[b], g_head).astype(jnp.bfloat16)
            key_term = (nn_product(dscores[b], q_head) * SCALE).astype(jnp.bfloat16)
            part = tn_product(dscores[b], k_all[b, head])
            dq_head = part if dq_head is None else dq_head + part
            if b == 1:
                own[0, head] = key_term
                own[1, head] = value_term
            else:
                sent[1 - b // 2, head, 0] = key_term
                sent[1 - b // 2, head, 1] = value_term
        dq_all[head] = (dq_head * SCALE).astype(jnp.bfloat16)
        for way in range(2):
            @pl.when(sends[way])
            def _():
                term_copy(head, way).start()
        out_copy(head, 0).start()

        @pl.when(head >= 2)
        def _():
            combine(head - 2)

        return carry

    lax.fori_loop(0, heads, one_head, 0)
    for head in range(max(heads - 2, 0), heads):
        combine(head)

    def finish(head, carry):
        for way in range(2):
            @pl.when(sends[way])
            def _():
                for copy in kv_copies(head, way):
                    copy.wait_send()
                term_copy(head, way).wait_send()
        for which in range(3):
            out_copy(head, which).wait()
        return carry

    lax.fori_loop(0, heads, finish, 0)


def place_kernel(*refs):
    for source, target in zip(refs[:3], refs[3:]):
        target[...] = source[...]


def per_device(queries, keys_in, values, grad_out, clip_ids):
    row_tok, width = queries.shape
    heads = width // HEAD_DIM
    shape = jax.ShapeDtypeStruct((row_tok, width), jnp.bfloat16)
    anywhere = pl.BlockSpec(memory_space=pl.ANY)
    low = jnp.bfloat16
    grads = pl.pallas_call(
        attention_kernel,
        out_shape=(shape, shape, shape),
        in_specs=[pl.BlockSpec(memory_space=pltpu.SMEM)] + [anywhere] * 4,
        out_specs=(anywhere, anywhere, anywhere),
        scratch_shapes=[
            pltpu.VMEM((heads, row_tok, HEAD_DIM), low),
            pltpu.VMEM((heads, row_tok, HEAD_DIM), low),
            pltpu.VMEM((3, heads, row_tok, HEAD_DIM), low),
            pltpu.VMEM((3, heads, row_tok, HEAD_DIM), low),
            pltpu.VMEM((2, heads, 2, row_tok, HEAD_DIM), low),
            pltpu.VMEM((2, heads, 2, row_tok, HEAD_DIM), low),
            pltpu.VMEM((2, heads, row_tok, HEAD_DIM), low),
            pltpu.VMEM((heads, row_tok, HEAD_DIM), low),
            pltpu.VMEM((3, row_tok, row_tok), jnp.float32),
            pltpu.VMEM((3, row_tok, row_tok), jnp.float32),
            pltpu.VMEM((3, row_tok, row_tok), low),
            pltpu.VMEM((3, row_tok, row_tok), low),
            pltpu.SemaphoreType.DMA((4, heads)),
            pltpu.SemaphoreType.DMA((2, heads, 2)),
            pltpu.SemaphoreType.DMA((2, heads, 2)),
            pltpu.SemaphoreType.DMA((2, heads)),
            pltpu.SemaphoreType.DMA((2, heads)),
            pltpu.SemaphoreType.DMA((3, heads)),
        ],
        compiler_params=pltpu.CompilerParams(
            collective_id=0, has_side_effects=True, vmem_limit_bytes=58 * 1024 * 1024
        ),
    )(clip_ids, queries, keys_in, values, grad_out)
    block = pl.BlockSpec((row_tok // 3, width), lambda step: (step, 0))
    return pl.pallas_call(
        place_kernel,
        grid=(3,),
        out_shape=(shape, shape, shape),
        in_specs=[block] * 3,
        out_specs=(block, block, block),
    )(*grads)


def solution(mesh):
    tokens = P(("groups", "ctx", "rep"), "head")
    return jax.shard_map(
        per_device,
        mesh=mesh,
        in_specs=(tokens, tokens, tokens, tokens, P("groups")),
        out_specs=(tokens, tokens, tokens),
        check_vma=False,
    )
```

```python
import functools
import math

import jax
import jax.numpy as jnp
from jax import lax
from jax.experimental import pallas as pl
from jax.experimental.pallas import tpu as pltpu
from jax.sharding import PartitionSpec as P

HEAD_DIM = 128
KEY_CHUNK = 32
LANES = 8
SCALE = HEAD_DIM ** -0.5
SCALE_LOG2 = SCALE * math.log2(math.e)
MESH = pl.DeviceIdType.MESH


def nt_product(left, right):
    return lax.dot_general(
        left, right, (((1,), (1,)), ((), ())), preferred_element_type=jnp.float32
    )


def tn_product(left, right):
    return lax.dot_general(
        left, right, (((0,), (0,)), ((), ())), preferred_element_type=jnp.float32
    )


def nn_product(left, right):
    return jnp.dot(left, right, preferred_element_type=jnp.float32)


def attention_kernel(
    clip_ref, q_hbm, k_hbm, v_hbm, g_hbm, dq_hbm, dk_hbm, dv_hbm,
    q_all, g_all, k_all, v_all, sent, got, own, dq_all,
    weights, dprobs, probs_low, dscores,
    load_sem, kv_send, kv_recv, term_send, term_recv, out_sem,
):
    heads, row_tok, _ = q_all.shape
    reps = lax.axis_size("rep")
    count = lax.axis_size("ctx") * reps
    position = lax.axis_index("ctx") * reps + lax.axis_index("rep")
    has_low, has_high = position > 0, position < count - 1

    def device(index):
        return {"ctx": index // reps, "rep": lax.rem(index, reps)}

    high = device(jnp.minimum(position + 1, count - 1))
    low = device(jnp.maximum(position - 1, 0))
    targets = (high, low)
    sends = (has_high, has_low)
    receives = (has_low, has_high)

    def strip(head):
        return pl.ds(pl.multiple_of(head * HEAD_DIM, HEAD_DIM), HEAD_DIM)

    def kv_copies(head, way):
        return [
            pltpu.make_async_remote_copy(
                src_ref=target.at[1, head],
                dst_ref=target.at[2 * way, head],
                send_sem=kv_send.at[way, head, which],
                recv_sem=kv_recv.at[way, head, which],
                device_id=targets[way],
                device_id_type=MESH,
            )
            for which, target in enumerate((k_all, v_all))
        ]

    def term_copy(head, way):
        return pltpu.make_async_remote_copy(
            src_ref=sent.at[way, head],
            dst_ref=got.at[way, head],
            send_sem=term_send.at[way, head],
            recv_sem=term_recv.at[way, head],
            device_id=targets[way],
            device_id_type=MESH,
        )

    def out_copy(head, which):
        columns = strip(head)
        source = (dq_all.at[head], own.at[0, head], own.at[1, head])[which]
        target = (dq_hbm, dk_hbm, dv_hbm)[which]
        return pltpu.make_async_copy(
            source, target.at[:, columns], out_sem.at[which, head]
        )

    def send_kv(head):
        for way in range(2):
            @pl.when(sends[way])
            def _():
                for copy in kv_copies(head, way):
                    copy.start()

    def loads(head):
        columns = strip(head)
        return [
            pltpu.make_async_copy(source.at[:, columns], target, load_sem.at[index, head])
            for index, (source, target) in enumerate(
                (
                    (k_hbm, k_all.at[1, head]),
                    (v_hbm, v_all.at[1, head]),
                    (q_hbm, q_all.at[head]),
                    (g_hbm, g_all.at[head]),
                )
            )
        ]

    barrier = pltpu.get_barrier_semaphore()
    for way in range(2):
        @pl.when(sends[way])
        def _():
            pl.semaphore_signal(barrier, inc=1, device_id=targets[way], device_id_type=MESH)
    for head in range(heads):
        for load in loads(head):
            load.start()
    pl.semaphore_wait(barrier, has_low.astype(jnp.int32) + has_high.astype(jnp.int32))
    for head in range(heads):
        for load in loads(head)[:2]:
            load.wait()
        if head < 2:
            send_kv(head)
    for way in range(2):
        @pl.when(jnp.logical_not(receives[way]))
        def _():
            k_all[2 * way] = jnp.zeros((heads, row_tok, HEAD_DIM), jnp.bfloat16)
            v_all[2 * way] = jnp.zeros((heads, row_tok, HEAD_DIM), jnp.bfloat16)
            got[way] = jnp.zeros((heads, 2, row_tok, HEAD_DIM), jnp.bfloat16)
    for head in range(heads):
        for load in loads(head)[2:]:
            load.wait()

    own_clip = clip_ref[position]
    low_clip = clip_ref[jnp.maximum(position - 1, 0)]
    high_clip = clip_ref[jnp.minimum(position + 1, count - 1)]
    biases = (
        jnp.where(has_low & (low_clip == own_clip), 0.0, -jnp.inf),
        0.0,
        jnp.where(has_high & (high_clip == own_clip), 0.0, -jnp.inf),
    )

    def combine(head):
        for way in range(2):
            @pl.when(receives[way])
            def _():
                term_copy(head, way).wait_recv()
        for which in range(2):
            total = own[which, head].astype(jnp.float32)
            for way in range(2):
                total = total + got[way, head, which].astype(jnp.float32)
            own[which, head] = total.astype(jnp.bfloat16)
            out_copy(head, 1 + which).start()

    def one_head(head, carry):
        for way in range(2):
            @pl.when(receives[way])
            def _():
                for copy in kv_copies(head, way):
                    copy.wait_recv()

        @pl.when(head + 2 < heads)
        def _():
            send_kv(head + 2)

        q_head, g_head = q_all[head], g_all[head]
        chunks = [pl.ds(start, KEY_CHUNK) for start in range(0, row_tok, KEY_CHUNK)]

        def folded(value, op):
            return op(value.reshape(KEY_CHUNK // LANES, LANES, row_tok), axis=0)

        top = None
        for b in range(3):
            weights[b] = nt_product(k_all[b, head], q_head)
            block_top = None
            for chunk in chunks:
                part = folded(weights[b, chunk, :], jnp.max)
                block_top = part if block_top is None else jnp.maximum(block_top, part)
            block_top = jnp.max(block_top, axis=0, keepdims=True) + biases[b]
            top = block_top if top is None else jnp.maximum(top, block_top)
        total = jnp.zeros((LANES, row_tok), jnp.float32)
        delta = jnp.zeros((LANES, row_tok), jnp.float32)
        for b in range(3):
            dprobs[b] = nt_product(v_all[b, head], g_head)
            shift = (top - biases[b]) * SCALE_LOG2
            for chunk in chunks:
                weight = jnp.exp2(weights[b, chunk, :] * SCALE_LOG2 - shift)
                weights[b, chunk, :] = weight
                total = total + folded(weight, jnp.sum)
                delta = delta + folded(weight * dprobs[b, chunk, :], jnp.sum)
        inverse = 1.0 / jnp.sum(total, axis=0, keepdims=True)
        delta = inverse * jnp.sum(delta, axis=0, keepdims=True)
        dq_head = None
        for b in (0, 2, 1):
            for chunk in chunks:
                probs = weights[b, chunk, :] * inverse
                probs_low[b, chunk, :] = probs.astype(jnp.bfloat16)
                dscores[b, chunk, :] = (probs * (dprobs[b, chunk, :] - delta)).astype(
                    jnp.bfloat16
                )
            value_term = nn_product(probs_low[b], g_head).astype(jnp.bfloat16)
            key_term = (nn_product(dscores[b], q_head) * SCALE).astype(jnp.bfloat16)
            part = tn_product(dscores[b], k_all[b, head])
            dq_head = part if dq_head is None else dq_head + part
            if b == 1:
                own[0, head] = key_term
                own[1, head] = value_term
            else:
                sent[1 - b // 2, head, 0] = key_term
                sent[1 - b // 2, head, 1] = value_term
        dq_all[head] = (dq_head * SCALE).astype(jnp.bfloat16)
        for way in range(2):
            @pl.when(sends[way])
            def _():
                term_copy(head, way).start()
        out_copy(head, 0).start()

        @pl.when(head >= 2)
        def _():
            combine(head - 2)

        return carry

    lax.fori_loop(0, heads, one_head, 0)
    for head in range(max(heads - 2, 0), heads):
        combine(head)

    def finish(head, carry):
        for way in range(2):
            @pl.when(sends[way])
            def _():
                for copy in kv_copies(head, way):
                    copy.wait_send()
                term_copy(head, way).wait_send()
        for which in range(3):
            out_copy(head, which).wait()
        return carry

    lax.fori_loop(0, heads, finish, 0)


def place_kernel(*refs):
    for source, target in zip(refs[:3], refs[3:]):
        target[...] = source[...]


def per_device(queries, keys_in, values, grad_out, clip_ids):
    row_tok, width = queries.shape
    heads = width // HEAD_DIM
    shape = jax.ShapeDtypeStruct((row_tok, width), jnp.bfloat16)
    anywhere = pl.BlockSpec(memory_space=pl.ANY)
    low = jnp.bfloat16
    grads = pl.pallas_call(
        attention_kernel,
        out_shape=(shape, shape, shape),
        in_specs=[pl.BlockSpec(memory_space=pltpu.SMEM)] + [anywhere] * 4,
        out_specs=(anywhere, anywhere, anywhere),
        scratch_shapes=[
            pltpu.VMEM((heads, row_tok, HEAD_DIM), low),
            pltpu.VMEM((heads, row_tok, HEAD_DIM), low),
            pltpu.VMEM((3, heads, row_tok, HEAD_DIM), low),
            pltpu.VMEM((3, heads, row_tok, HEAD_DIM), low),
            pltpu.VMEM((2, heads, 2, row_tok, HEAD_DIM), low),
            pltpu.VMEM((2, heads, 2, row_tok, HEAD_DIM), low),
            pltpu.VMEM((2, heads, row_tok, HEAD_DIM), low),
            pltpu.VMEM((heads, row_tok, HEAD_DIM), low),
            pltpu.VMEM((3, row_tok, row_tok), jnp.float32),
            pltpu.VMEM((3, row_tok, row_tok), jnp.float32),
            pltpu.VMEM((3, row_tok, row_tok), low),
            pltpu.VMEM((3, row_tok, row_tok), low),
            pltpu.SemaphoreType.DMA((4, heads)),
            pltpu.SemaphoreType.DMA((2, heads, 2)),
            pltpu.SemaphoreType.DMA((2, heads, 2)),
            pltpu.SemaphoreType.DMA((2, heads)),
            pltpu.SemaphoreType.DMA((2, heads)),
            pltpu.SemaphoreType.DMA((3, heads)),
        ],
        compiler_params=pltpu.CompilerParams(
            collective_id=0, has_side_effects=True, vmem_limit_bytes=58 * 1024 * 1024
        ),
    )(clip_ids, queries, keys_in, values, grad_out)
    block = pl.BlockSpec((row_tok // 6, width), lambda step: (step, 0))
    return pl.pallas_call(
        place_kernel,
        grid=(6,),
        out_shape=(shape, shape, shape),
        in_specs=[block] * 3,
        out_specs=(block, block, block),
    )(*grads)


def solution(mesh):
    tokens = P(("groups", "ctx", "rep"), "head")
    return jax.shard_map(
        per_device,
        mesh=mesh,
        in_specs=(tokens, tokens, tokens, tokens, P("groups")),
        out_specs=(tokens, tokens, tokens),
        check_vma=False,
    )
```
